32 devices in a mesh: light: 8 (over z, y), depth: 2 (over core), tile: 2 (over x).
Axes of the slice: x: 2, y: 2, z: 4, core: 2. Of those that a mesh axis runs over, the one named last changes fastest.
Arguments:
- density: float32 [256, 128, 1024], P('light', 'depth', 'tile'), may hold values from 0.05 to 2
- extinction: float32 [3], replicated, may hold values from 1 to 4
- sun_colour: float32 [3], replicated, may hold values from 1 to 3
- sky_colour: float32 [3], replicated, may hold values from 0.2 to 2
Outputs:
- image: float32 [3, 256, 1024], P(None, ('light', 'depth'), 'tile')
- transmittance: float32 [3, 256, 1024], P(None, ('light', 'depth'), 'tile')
The draws below stay inside these ranges and needn't reach their ends.
All inputs are finite; a program needn't handle non-finite values.
Results may differ from the reference program's by a relative error of at most 0.0003.
Values sent between devices are 32-bit elements; how exact they have to be, the bound alone decides.
A program may use at most 64 MiB of HBM per device.

```python
import math
import jax
import jax.numpy as jnp
from jax import lax

BZ = 512
COLOURS = 3
NX = 256
NY = 128
NZ = 1024


def levels(rng, extent, cuts, low, largest):
    factor_of, own = 1.0, jax.random.fold_in(rng, 6)
    for position, blocks in cuts:
        steps = jnp.exp(jax.random.uniform(jax.random.fold_in(own, position), (blocks,), jnp.float32, low / len(cuts), largest / len(cuts)))
        factor_of = factor_of * jnp.repeat(steps, extent[position] // blocks).reshape([-1 if axis == position else 1 for axis in range(len(extent))])
    return factor_of


def setup_inputs(seed: int = 0) -> dict:
    streams_of = jax.random.split(jax.random.key(seed), 5)
    return {
        "density": jnp.clip(jnp.exp(math.log(2.0) - 3.6888794 * jax.random.uniform(streams_of[0], (NX, NY, NZ), jnp.float32) ** levels(streams_of[0], (NX, NY, NZ), ((0, 8), (1, 2), (2, 2)), -0.2, 0.2)), 0.05, 2.0),
        "extinction": jnp.clip(jnp.exp(jax.random.uniform(streams_of[1], (COLOURS,), jnp.float32, math.log(1.0), math.log(4.0))), 1.0, 4.0),
        "sun_colour": jnp.clip(jax.random.uniform(streams_of[2], (COLOURS,), jnp.float32, 1.0, 3.0), 1.0, 3.0),
        "sky_colour": jnp.clip(jax.random.uniform(streams_of[3], (COLOURS,), jnp.float32, 0.2, 2.0), 0.2, 2.0),
    }


def render_block(block, extinction, sun_colour, sky_colour):
    full_x = block.shape[0]
    full_y = block.shape[1]
    sun_depth = (jnp.cumsum(block, axis=0) - 0.5 * block) / full_x
    view_depth = (jnp.cumsum(block, axis=1) - block) / full_y
    column_total = jnp.sum(block, axis=1) / full_y
    images = []
    passes = []
    for colour in range(3):
        radiance = sun_colour[colour] * jnp.exp(-extinction[colour] * sun_depth)
        opacity = -jnp.expm1(-extinction[colour] * block / full_y)
        weight = jnp.exp(-extinction[colour] * view_depth)
        summed = jnp.sum(weight * opacity * radiance, axis=1)
        passing = jnp.exp(-extinction[colour] * column_total)
        images.append(summed + sky_colour[colour] * passing)
        passes.append(passing)
    return jnp.stack(images), jnp.stack(passes)


def reference(density, extinction, sun_colour, sky_colour):
    width = BZ // max(1, BZ // 128)
    count = NZ // width

    def one_block(index):
        block = lax.dynamic_slice_in_dim(density, (index * width).astype(jnp.int32), width, 2)
        return render_block(block, extinction, sun_colour, sky_colour)

    images, passes = lax.map(one_block, jnp.arange(count, dtype=jnp.int32))
    image = jnp.transpose(images, (1, 2, 0, 3)).reshape(3, NX, NZ)
    transmittance = jnp.transpose(passes, (1, 2, 0, 3)).reshape(3, NX, NZ)
    return image, transmittance
```

```python
import functools
import math

import jax
import jax.numpy as jnp
from jax import lax
from jax.experimental import pallas as pl
from jax.experimental.pallas import tpu as pltpu
from jax.sharding import PartitionSpec as P

LANES = 128
ROWS = 8
LOG2E = math.log2(math.e)
MESH = pl.DeviceIdType.MESH


def kernel(light_count, full_x, full_y, density, extinction_in, sun_in, sky_in, image, trans,
           extinction, sun_colour, sky_colour, dens, weight, front, own, chain_in, side_in, before, share, share_in,
           small_sem, load_sem, chain_send, chain_recv, side_send, side_recv, share_send, share_recv):
    chunks, size_x, size_y, _ = dens.shape
    seg = size_y // ROWS
    half = size_x // 2
    pair = 2 if light_count % 2 == 0 else 1
    length = light_count // pair
    light = lax.axis_index("light")
    depth = lax.axis_index("depth")
    level, side = light // pair, light % pair
    last = level == length - 1
    partner = light + 1 - 2 * side
    other = 1 - depth

    sends_chain = level < length - 1
    gets_chain = level > 0
    if pair == 2:
        sends_side = jnp.logical_or(side == 0, level > 0)
        gets_side = jnp.logical_or(side == 1, level > 0)

    def load(j):
        return pltpu.make_async_copy(density.at[:, :, pl.ds(j * LANES, LANES)], dens.at[j], load_sem.at[j])

    def chain(j):
        return pltpu.make_async_remote_copy(
            own.at[j], chain_in.at[j], chain_send.at[j], chain_recv.at[j],
            device_id={"light": light + pair}, device_id_type=MESH)

    def side_copy(j, source):
        return pltpu.make_async_remote_copy(
            source.at[j], side_in.at[j], side_send.at[j], side_recv.at[j],
            device_id={"light": partner}, device_id_type=MESH)

    def share_copy(j):
        return pltpu.make_async_remote_copy(
            share.at[j, :, pl.ds(pl.multiple_of(other * half, half), half)], share_in.at[j],
            share_send.at[j], share_recv.at[j],
            device_id={"depth": other}, device_id_type=MESH)

    for j in range(chunks):
        load(j).start()
    colours = [pltpu.make_async_copy(a, b, small_sem.at[i]) for i, (a, b) in enumerate(
        ((extinction_in, extinction), (sun_in, sun_colour), (sky_in, sky_colour)))]
    for copy in colours:
        copy.start()

    barrier = pltpu.get_barrier_semaphore()
    pl.semaphore_signal(barrier, inc=1, device_id={"depth": other}, device_id_type=MESH)
    if pair == 2:
        pl.semaphore_signal(barrier, inc=1, device_id={"light": partner}, device_id_type=MESH)

    @pl.when(sends_chain)
    def _():
        pl.semaphore_signal(barrier, inc=1, device_id={"light": light + pair}, device_id_type=MESH)

    @pl.when(gets_chain)
    def _():
        pl.semaphore_signal(barrier, inc=1, device_id={"light": light - pair}, device_id_type=MESH)

    pl.semaphore_wait(barrier, pair + jnp.minimum(level, 1) + jnp.minimum(length - 1 - level, 1))

    def cells(j, x):
        return [dens[j, x, pl.ds(s, ROWS, stride=seg), :] for s in range(seg)]

    def send_sums(j):
        @pl.when(sends_chain)
        def _():
            chain(j).start()

        if pair == 2:
            @pl.when(side == 0)
            def _():
                side_copy(j, own).start()

    for j in range(chunks):
        load(j).wait()

        def sums(x, total):
            d = cells(j, x)
            front[j, x] = functools.reduce(jnp.add, d)
            return tuple(t + v for t, v in zip(total, d))

        zero = jnp.zeros((ROWS, LANES), jnp.float32)
        total = lax.fori_loop(0, size_x, sums, (zero,) * seg, unroll=4)
        for s in range(seg):
            own[j, s] = total[s]

        @pl.when(level == 0)
        def _():
            send_sums(j)

    row = lax.broadcasted_iota(jnp.int32, (ROWS, LANES), 0)

    def shifted(v, n):
        return jnp.where(row >= n, pltpu.roll(v, n, 0), 0.0)

    def scan_group(g, carry):
        j, b = g // (size_x // ROWS), g % (size_x // ROWS)
        x0 = pl.multiple_of(b * ROWS, ROWS)
        group = front[j, pl.ds(x0, ROWS)]
        share[j, 3, pl.ds(x0, ROWS)] = jnp.sum(group, axis=1)
        for i in range(ROWS):
            v = shifted(group[i], 1)
            n = 1
            while n < ROWS:
                v = v + shifted(v, n)
                n *= 2
            front[j, x0 + i] = v
        return carry

    lax.fori_loop(0, chunks * (size_x // ROWS), scan_group, 0)

    for copy in colours:
        copy.wait()
    half_step = [extinction[c] * (-LOG2E / (2 * full_x)) for c in range(3)]
    view_step = [extinction[c] * (-LOG2E / full_y) for c in range(3)]
    sun_step = [extinction[c] * (-LOG2E / full_x) for c in range(3)]
    ratio = 2 * full_x // full_y
    squares = ratio.bit_length() - 1
    by_squares = ratio * full_y == 2 * full_x and ratio == 1 << squares and squares <= 3

    def weigh(j, carry):
        def step(x, lit):
            d = cells(j, x)
            e = front[j, x]
            after = []
            for c in range(3):
                seen = jnp.exp2(view_step[c] * e)
                for s in range(seg):
                    q = jnp.exp2(half_step[c] * d[s])
                    if by_squares:
                        a = q
                        for _ in range(squares):
                            a = a * a
                    else:
                        a = jnp.exp2(view_step[c] * d[s])
                    r = lit[c * seg + s] * q
                    after.append(r * q)
                    behind = seen * a
                    weight[j, c, x, s] = (seen - behind) * r
                    seen = behind
            return tuple(after)

        one = jnp.ones((ROWS, LANES), jnp.float32)
        lax.fori_loop(0, size_x, step, (one,) * (3 * seg))
        return carry

    early = jnp.minimum(level, chunks)
    lax.fori_loop(0, early, weigh, 0)

    for j in range(chunks):
        @pl.when(gets_chain)
        def _():
            chain(j).wait_recv()
            if pair == 2:
                @pl.when(side == 1)
                def _():
                    side_copy(j, chain_in).start()
            own[j] = own[j] + chain_in[j]
            send_sums(j)

    lax.fori_loop(early, chunks, weigh, 0)

    def finish_rows(j, block):
        for c in range(3):
            g = [sun_colour[c] * jnp.exp2(sun_step[c] * before[s]) for s in range(seg)]
            for b in range(half // ROWS):
                x0 = block * half + b * ROWS
                parts = []
                for i in range(ROWS):
                    acc = weight[j, c, x0 + i, 0] * g[0]
                    for s in range(1, seg):
                        acc = acc + weight[j, c, x0 + i, s] * g[s]
                    parts.append(acc)
                share[j, c, pl.ds(pl.multiple_of(x0, ROWS), ROWS)] = jnp.sum(jnp.stack(parts), axis=1)

    def prepare(j):
        before[...] = jnp.zeros_like(before)

        @pl.when(gets_chain)
        def _():
            before[...] = chain_in[j]

        if pair == 2:
            @pl.when(gets_side)
            def _():
                side_copy(j, own).wait_recv()
                before[...] = before[...] + side_in[j]

    def combine(j):
        share_copy(j).wait_recv()
        mine = pl.ds(pl.multiple_of(depth * half, half), half)
        lanes = pl.ds(j * LANES, LANES)
        near = depth == 0
        view, view_in = share[j, 3, mine], share_in[j, 3]
        view_front = jnp.where(near, view, view_in)
        for c in range(3):
            here, there = share[j, c, mine], share_in[j, c]
            first, second = jnp.where(near, here, there), jnp.where(near, there, here)
            passing = jnp.exp2(view_step[c] * (view + view_in))
            trans[c, :, lanes] = passing
            image[c, :, lanes] = (first + jnp.exp2(view_step[c] * view_front) * second) + sky_colour[c] * passing

    for j in range(chunks):
        prepare(j)
        finish_rows(j, other)
        share_copy(j).start()
        finish_rows(j, depth)
    for j in range(chunks):
        combine(j)

    for j in range(chunks):
        share_copy(j).wait_send()

        @pl.when(sends_chain)
        def _():
            chain(j).wait_send()

        if pair == 2:
            @pl.when(sends_side)
            def _():
                side_copy(j, own).wait_send()


def per_device(mesh_shape, density, extinction, sun_colour, sky_colour):
    light_count, depth_count = mesh_shape["light"], mesh_shape["depth"]
    size_x, size_y, size_z = density.shape
    assert depth_count == 2
    chunks, seg, half = size_z // LANES, size_y // ROWS, size_x // 2
    out = jax.ShapeDtypeStruct((3, half, size_z), jnp.float32)
    vmem = functools.partial(pltpu.VMEM, dtype=jnp.float32)
    tile = (ROWS, LANES)
    dma = pltpu.SemaphoreType.DMA((chunks,))
    hbm = pl.BlockSpec(memory_space=pltpu.HBM)
    small = pltpu.SMEM((3,), jnp.float32)
    whole = pl.BlockSpec(memory_space=pltpu.VMEM)
    return pl.pallas_call(
        functools.partial(kernel, light_count, size_x * light_count, size_y * depth_count),
        out_shape=(out, out),
        in_specs=[hbm] * 4,
        out_specs=(whole, whole),
        scratch_shapes=[small] * 3 + [
            vmem((chunks, size_x, size_y, LANES)),
            vmem((chunks, 3, size_x, seg) + tile),
            vmem((chunks, size_x) + tile),
            vmem((chunks, seg) + tile),
            vmem((chunks, seg) + tile),
            vmem((chunks, seg) + tile),
            vmem((seg,) + tile),
            vmem((chunks, 4, size_x, LANES)),
            vmem((chunks, 4, half, LANES)),
        ] + [pltpu.SemaphoreType.DMA((3,))] + [dma] * 7,
        compiler_params=pltpu.CompilerParams(collective_id=0, has_side_effects=True, vmem_limit_bytes=48 * 2**20),
    )(density, extinction, sun_colour, sky_colour)


def solution(mesh):
    return jax.shard_map(
        functools.partial(per_device, dict(mesh.shape)),
        mesh=mesh,
        in_specs=(P("light", "depth", "tile"), P(), P(), P()),
        out_specs=(P(None, ("light", "depth"), "tile"), P(None, ("light", "depth"), "tile")),
        check_vma=False,
    )
```

```python
import functools
import math

import jax
import jax.numpy as jnp
from jax import lax
from jax.experimental import pallas as pl
from jax.experimental.pallas import tpu as pltpu
from jax.sharding import PartitionSpec as P

LANES = 128
ROWS = 8
LOG2E = math.log2(math.e)
MESH = pl.DeviceIdType.MESH


def kernel(light_count, full_x, full_y, density, extinction_in, sun_in, image, column,
           extinction, sun_colour, dens, weight, front, own, chain_in, side_in, before, share, share_in,
           small_sem, load_sem, chain_send, chain_recv, side_send, side_recv, share_send, share_recv):
    chunks, size_x, size_y, _ = dens.shape
    seg = size_y // ROWS
    half = size_x // 2
    pair = 2 if light_count % 2 == 0 else 1
    length = light_count // pair
    light = lax.axis_index("light")
    depth = lax.axis_index("depth")
    level, side = light // pair, light % pair
    last = level == length - 1
    partner = light + 1 - 2 * side
    other = 1 - depth

    sends_chain = level < length - 1
    gets_chain = level > 0
    if pair == 2:
        sends_side = jnp.logical_or(side == 0, level > 0)
        gets_side = jnp.logical_or(side == 1, level > 0)

    def load(j):
        return pltpu.make_async_copy(density.at[:, :, pl.ds(j * LANES, LANES)], dens.at[j], load_sem.at[j])

    def chain(j):
        return pltpu.make_async_remote_copy(
            own.at[j], chain_in.at[j], chain_send.at[j], chain_recv.at[j],
            device_id={"light": light + pair}, device_id_type=MESH)

    def side_copy(j, source):
        return pltpu.make_async_remote_copy(
            source.at[j], side_in.at[j], side_send.at[j], side_recv.at[j],
            device_id={"light": partner}, device_id_type=MESH)

    def share_copy(j):
        return pltpu.make_async_remote_copy(
            share.at[j, :, pl.ds(pl.multiple_of(other * half, half), half)], share_in.at[j],
            share_send.at[j], share_recv.at[j],
            device_id={"depth": other}, device_id_type=MESH)

    for j in range(chunks):
        load(j).start()
    colours = [pltpu.make_async_copy(a, b, small_sem.at[i]) for i, (a, b) in enumerate(
        ((extinction_in, extinction), (sun_in, sun_colour)))]
    for copy in colours:
        copy.start()

    barrier = pltpu.get_barrier_semaphore()
    pl.semaphore_signal(barrier, inc=1, device_id={"depth": other}, device_id_type=MESH)
    if pair == 2:
        pl.semaphore_signal(barrier, inc=1, device_id={"light": partner}, device_id_type=MESH)

    @pl.when(sends_chain)
    def _():
        pl.semaphore_signal(barrier, inc=1, device_id={"light": light + pair}, device_id_type=MESH)

    @pl.when(gets_chain)
    def _():
        pl.semaphore_signal(barrier, inc=1, device_id={"light": light - pair}, device_id_type=MESH)

    pl.semaphore_wait(barrier, pair + jnp.minimum(level, 1) + jnp.minimum(length - 1 - level, 1))

    def cells(j, x):
        return [dens[j, x, pl.ds(s, ROWS, stride=seg), :] for s in range(seg)]

    def send_sums(j):
        @pl.when(sends_chain)
        def _():
            chain(j).start()

        if pair == 2:
            @pl.when(side == 0)
            def _():
                side_copy(j, own).start()

    for j in range(chunks):
        load(j).wait()

        def sums(x, total):
            d = cells(j, x)
            front[j, x] = functools.reduce(jnp.add, d)
            return tuple(t + v for t, v in zip(total, d))

        zero = jnp.zeros((ROWS, LANES), jnp.float32)
        total = lax.fori_loop(0, size_x, sums, (zero,) * seg, unroll=4)
        for s in range(seg):
            own[j, s] = total[s]

        @pl.when(level == 0)
        def _():
            send_sums(j)

    row = lax.broadcasted_iota(jnp.int32, (ROWS, LANES), 0)

    def shifted(v, n):
        return jnp.where(row >= n, pltpu.roll(v, n, 0), 0.0)

    def scan_group(g, carry):
        j, b = g // (size_x // ROWS), g % (size_x // ROWS)
        x0 = pl.multiple_of(b * ROWS, ROWS)
        group = front[j, pl.ds(x0, ROWS)]
        share[j, 3, pl.ds(x0, ROWS)] = jnp.sum(group, axis=1)
        for i in range(ROWS):
            v = shifted(group[i], 1)
            n = 1
            while n < ROWS:
                v = v + shifted(v, n)
                n *= 2
            front[j, x0 + i] = v
        return carry

    lax.fori_loop(0, chunks * (size_x // ROWS), scan_group, 0)

    for copy in colours:
        copy.wait()
    half_step = [extinction[c] * (-LOG2E / (2 * full_x)) for c in range(3)]
    view_step = [extinction[c] * (-LOG2E / full_y) for c in range(3)]
    sun_step = [extinction[c] * (-LOG2E / full_x) for c in range(3)]
    ratio = 2 * full_x // full_y
    squares = ratio.bit_length() - 1
    by_squares = ratio * full_y == 2 * full_x and ratio == 1 << squares and squares <= 3

    def weigh(j, carry):
        def step(x, lit):
            d = cells(j, x)
            e = front[j, x]
            after = []
            for c in range(3):
                seen = jnp.exp2(view_step[c] * e)
                for s in range(seg):
                    q = jnp.exp2(half_step[c] * d[s])
                    if by_squares:
                        a = q
                        for _ in range(squares):
                            a = a * a
                    else:
                        a = jnp.exp2(view_step[c] * d[s])
                    r = lit[c * seg + s] * q
                    after.append(r * q)
                    behind = seen * a
                    weight[j, c, x, s] = (seen - behind) * r
                    seen = behind
            return tuple(after)

        one = jnp.ones((ROWS, LANES), jnp.float32)
        lax.fori_loop(0, size_x, step, (one,) * (3 * seg))
        return carry

    early = jnp.minimum(level, chunks)
    lax.fori_loop(0, early, weigh, 0)

    for j in range(chunks):
        @pl.when(gets_chain)
        def _():
            chain(j).wait_recv()
            if pair == 2:
                @pl.when(side == 1)
                def _():
                    side_copy(j, chain_in).start()
            own[j] = own[j] + chain_in[j]
            send_sums(j)

    lax.fori_loop(early, chunks, weigh, 0)

    def finish_rows(j, block):
        for c in range(3):
            g = [sun_colour[c] * jnp.exp2(sun_step[c] * before[s]) for s in range(seg)]
            for b in range(half // ROWS):
                x0 = block * half + b * ROWS
                parts = []
                for i in range(ROWS):
                    acc = weight[j, c, x0 + i, 0] * g[0]
                    for s in range(1, seg):
                        acc = acc + weight[j, c, x0 + i, s] * g[s]
                    parts.append(acc)
                share[j, c, pl.ds(pl.multiple_of(x0, ROWS), ROWS)] = jnp.sum(jnp.stack(parts), axis=1)

    def prepare(j):
        before[...] = jnp.zeros_like(before)

        @pl.when(gets_chain)
        def _():
            before[...] = chain_in[j]

        if pair == 2:
            @pl.when(gets_side)
            def _():
                side_copy(j, own).wait_recv()
                before[...] = before[...] + side_in[j]

    def combine(j):
        share_copy(j).wait_recv()
        mine = pl.ds(pl.multiple_of(depth * half, half), half)
        lanes = pl.ds(j * LANES, LANES)
        near = depth == 0
        view, view_in = share[j, 3, mine], share_in[j, 3]
        view_front = jnp.where(near, view, view_in)
        for c in range(3):
            here, there = share[j, c, mine], share_in[j, c]
            first, second = jnp.where(near, here, there), jnp.where(near, there, here)
            image[c, :, lanes] = first + jnp.exp2(view_step[c] * view_front) * second
        column[:, lanes] = view + view_in

    for j in range(chunks):
        prepare(j)
        finish_rows(j, other)
        share_copy(j).start()
        finish_rows(j, depth)
    for j in range(chunks):
        combine(j)

    for j in range(chunks):
        share_copy(j).wait_send()

        @pl.when(sends_chain)
        def _():
            chain(j).wait_send()

        if pair == 2:
            @pl.when(sends_side)
            def _():
                side_copy(j, own).wait_send()


def per_device(mesh_shape, density, extinction, sun_colour, sky_colour):
    light_count, depth_count = mesh_shape["light"], mesh_shape["depth"]
    size_x, size_y, size_z = density.shape
    assert depth_count == 2
    chunks, seg, half = size_z // LANES, size_y // ROWS, size_x // 2
    out = jax.ShapeDtypeStruct((3, half, size_z), jnp.float32)
    vmem = functools.partial(pltpu.VMEM, dtype=jnp.float32)
    tile = (ROWS, LANES)
    dma = pltpu.SemaphoreType.DMA((chunks,))
    hbm = pl.BlockSpec(memory_space=pltpu.HBM)
    small = pltpu.SMEM((3,), jnp.float32)
    whole = pl.BlockSpec(memory_space=pltpu.VMEM)
    image, column = pl.pallas_call(
        functools.partial(kernel, light_count, size_x * light_count, size_y * depth_count),
        out_shape=(out, jax.ShapeDtypeStruct((half, size_z), jnp.float32)),
        in_specs=[hbm] * 3,
        out_specs=(whole, whole),
        scratch_shapes=[small] * 2 + [
            vmem((chunks, size_x, size_y, LANES)),
            vmem((chunks, 3, size_x, seg) + tile),
            vmem((chunks, size_x) + tile),
            vmem((chunks, seg) + tile),
            vmem((chunks, seg) + tile),
            vmem((chunks, seg) + tile),
            vmem((seg,) + tile),
            vmem((chunks, 4, size_x, LANES)),
            vmem((chunks, 4, half, LANES)),
        ] + [pltpu.SemaphoreType.DMA((2,))] + [dma] * 7,
        compiler_params=pltpu.CompilerParams(collective_id=0, has_side_effects=True, vmem_limit_bytes=67043328),
    )(density, extinction, sun_colour)
    trans = jnp.exp(extinction[:, None, None] * (column / -(size_y * depth_count)))
    return image + sky_colour[:, None, None] * trans, trans


def solution(mesh):
    return jax.shard_map(
        functools.partial(per_device, dict(mesh.shape)),
        mesh=mesh,
        in_specs=(P("light", "depth", "tile"), P(), P(), P()),
        out_specs=(P(None, ("light", "depth"), "tile"), P(None, ("light", "depth"), "tile")),
        check_vma=False,
    )
```

```python
import functools
import math

import jax
import jax.numpy as jnp
from jax import lax
from jax.experimental import pallas as pl
from jax.experimental.pallas import tpu as pltpu
from jax.sharding import PartitionSpec as P

LANES = 128
ROWS = 8
LOG2E = math.log2(math.e)
MESH = pl.DeviceIdType.MESH


def kernel(light_count, full_x, full_y, density, extinction_in, sun_in, image, column,
           extinction, sun_colour, dens, weight, front, own, chain_in, side_in, before, share, share_in,
           small_sem, load_sem, chain_send, chain_recv, side_send, side_recv, share_send, share_recv):
    chunks, size_x, size_y, _ = dens.shape
    seg = size_y // ROWS
    half = size_x // 2
    pair = 2 if light_count % 2 == 0 else 1
    length = light_count // pair
    light = lax.axis_index("light")
    depth = lax.axis_index("depth")
    level, side = light // pair, light % pair
    last = level == length - 1
    partner = light + 1 - 2 * side
    other = 1 - depth

    sends_chain = level < length - 1
    gets_chain = level > 0
    if pair == 2:
        sends_side = jnp.logical_or(side == 0, level > 0)
        gets_side = jnp.logical_or(side == 1, level > 0)

    def load(j):
        return pltpu.make_async_copy(density.at[:, :, pl.ds(j * LANES, LANES)], dens.at[j], load_sem.at[j])

    def chain(j):
        return pltpu.make_async_remote_copy(
            own.at[j], chain_in.at[j], chain_send.at[j], chain_recv.at[j],
            device_id={"light": light + pair}, device_id_type=MESH)

    def side_copy(j, source):
        return pltpu.make_async_remote_copy(
            source.at[j], side_in.at[j], side_send.at[j], side_recv.at[j],
            device_id={"light": partner}, device_id_type=MESH)

    def share_copy(j):
        return pltpu.make_async_remote_copy(
            share.at[j, :, pl.ds(pl.multiple_of(other * half, half), half)], share_in.at[j],
            share_send.at[j], share_recv.at[j],
            device_id={"depth": other}, device_id_type=MESH)

    for j in range(chunks):
        load(j).start()
    colours = [pltpu.make_async_copy(a, b, small_sem.at[i]) for i, (a, b) in enumerate(
        ((extinction_in, extinction), (sun_in, sun_colour)))]
    for copy in colours:
        copy.start()

    barrier = pltpu.get_barrier_semaphore()
    pl.semaphore_signal(barrier, inc=1, device_id={"depth": other}, device_id_type=MESH)
    if pair == 2:
        pl.semaphore_signal(barrier, inc=1, device_id={"light": partner}, device_id_type=MESH)

    @pl.when(sends_chain)
    def _():
        pl.semaphore_signal(barrier, inc=1, device_id={"light": light + pair}, device_id_type=MESH)

    @pl.when(gets_chain)
    def _():
        pl.semaphore_signal(barrier, inc=1, device_id={"light": light - pair}, device_id_type=MESH)

    pl.semaphore_wait(barrier, pair + jnp.minimum(level, 1) + jnp.minimum(length - 1 - level, 1))

    def cells(j, x):
        return [dens[j, x, pl.ds(s, ROWS, stride=seg), :] for s in range(seg)]

    def send_sums(j):
        @pl.when(sends_chain)
        def _():
            chain(j).start()

        if pair == 2:
            @pl.when(side == 0)
            def _():
                side_copy(j, own).start()

    for j in range(chunks):
        load(j).wait()

        def sums(x, total):
            d = cells(j, x)
            front[j, x] = functools.reduce(jnp.add, d)
            return tuple(t + v for t, v in zip(total, d))

        zero = jnp.zeros((ROWS, LANES), jnp.float32)
        total = lax.fori_loop(0, size_x, sums, (zero,) * seg, unroll=4)
        for s in range(seg):
            own[j, s] = total[s]

        @pl.when(level == 0)
        def _():
            send_sums(j)

    row = lax.broadcasted_iota(jnp.int32, (ROWS, LANES), 0)

    def shifted(v, n):
        return jnp.where(row >= n, pltpu.roll(v, n, 0), 0.0)

    def scan_group(g, carry):
        j, b = g // (size_x // ROWS), g % (size_x // ROWS)
        x0 = pl.multiple_of(b * ROWS, ROWS)
        group = front[j, pl.ds(x0, ROWS)]
        share[j, 3, pl.ds(x0, ROWS)] = jnp.sum(group, axis=1)
        for i in range(ROWS):
            v = shifted(group[i], 1)
            n = 1
            while n < ROWS:
                v = v + shifted(v, n)
                n *= 2
            front[j, x0 + i] = v
        return carry

    lax.fori_loop(0, chunks * (size_x // ROWS), scan_group, 0)

    for copy in colours:
        copy.wait()
    half_step = [extinction[c] * (-LOG2E / (2 * full_x)) for c in range(3)]
    view_step = [extinction[c] * (-LOG2E / full_y) for c in range(3)]
    sun_step = [extinction[c] * (-LOG2E / full_x) for c in range(3)]
    ratio = 2 * full_x // full_y
    squares = ratio.bit_length() - 1
    by_squares = ratio * full_y == 2 * full_x and ratio == 1 << squares and squares <= 3

    def weigh(j, carry):
        def step(x, lit):
            d = cells(j, x)
            e = front[j, x]
            after = []
            for c in range(3):
                seen = jnp.exp2(view_step[c] * e)
                for s in range(seg):
                    q = jnp.exp2(half_step[c] * d[s])
                    if by_squares:
                        a = q
                        for _ in range(squares):
                            a = a * a
                    else:
                        a = jnp.exp2(view_step[c] * d[s])
                    r = lit[c * seg + s] * q
                    after.append(r * q)
                    behind = seen * a
                    weight[j, c, x, s] = (seen - behind) * r
                    seen = behind
            return tuple(after)

        one = jnp.ones((ROWS, LANES), jnp.float32)
        lax.fori_loop(0, size_x, step, (one,) * (3 * seg), unroll=2)
        return carry

    early = jnp.minimum(level, chunks)
    lax.fori_loop(0, early, weigh, 0)

    for j in range(chunks):
        @pl.when(gets_chain)
        def _():
            chain(j).wait_recv()
            if pair == 2:
                @pl.when(side == 1)
                def _():
                    side_copy(j, chain_in).start()
            own[j] = own[j] + chain_in[j]
            send_sums(j)

    lax.fori_loop(early, chunks, weigh, 0)

    def finish_rows(j, block):
        for c in range(3):
            g = [sun_colour[c] * jnp.exp2(sun_step[c] * before[s]) for s in range(seg)]
            for b in range(half // ROWS):
                x0 = block * half + b * ROWS
                parts = []
                for i in range(ROWS):
                    acc = weight[j, c, x0 + i, 0] * g[0]
                    for s in range(1, seg):
                        acc = acc + weight[j, c, x0 + i, s] * g[s]
                    parts.append(acc)
                share[j, c, pl.ds(pl.multiple_of(x0, ROWS), ROWS)] = jnp.sum(jnp.stack(parts), axis=1)

    def prepare(j):
        before[...] = jnp.zeros_like(before)

        @pl.when(gets_chain)
        def _():
            before[...] = chain_in[j]

        if pair == 2:
            @pl.when(gets_side)
            def _():
                side_copy(j, own).wait_recv()
                before[...] = before[...] + side_in[j]

    def combine(j):
        share_copy(j).wait_recv()
        mine = pl.ds(pl.multiple_of(depth * half, half), half)
        lanes = pl.ds(j * LANES, LANES)
        near = depth == 0
        view, view_in = share[j, 3, mine], share_in[j, 3]
        view_front = jnp.where(near, view, view_in)
        for c in range(3):
            here, there = share[j, c, mine], share_in[j, c]
            first, second = jnp.where(near, here, there), jnp.where(near, there, here)
            image[c, :, lanes] = first + jnp.exp2(view_step[c] * view_front) * second
        column[:, lanes] = (view + view_in) * (-1.0 / full_y)

    for j in range(chunks):
        prepare(j)
        finish_rows(j, other)
        share_copy(j).start()
        finish_rows(j, depth)
    for j in range(chunks):
        combine(j)

    for j in range(chunks):
        share_copy(j).wait_send()

        @pl.when(sends_chain)
        def _():
            chain(j).wait_send()

        if pair == 2:
            @pl.when(sends_side)
            def _():
                side_copy(j, own).wait_send()


def per_device(mesh_shape, density, extinction, sun_colour, sky_colour):
    light_count, depth_count = mesh_shape["light"], mesh_shape["depth"]
    size_x, size_y, size_z = density.shape
    assert depth_count == 2
    chunks, seg, half = size_z // LANES, size_y // ROWS, size_x // 2
    out = jax.ShapeDtypeStruct((3, half, size_z), jnp.float32)
    vmem = functools.partial(pltpu.VMEM, dtype=jnp.float32)
    tile = (ROWS, LANES)
    dma = pltpu.SemaphoreType.DMA((chunks,))
    hbm = pl.BlockSpec(memory_space=pltpu.HBM)
    small = pltpu.SMEM((3,), jnp.float32)
    whole = pl.BlockSpec(memory_space=pltpu.VMEM)
    image, column = pl.pallas_call(
        functools.partial(kernel, light_count, size_x * light_count, size_y * depth_count),
        out_shape=(out, jax.ShapeDtypeStruct((half, size_z), jnp.float32)),
        in_specs=[hbm] * 3,
        out_specs=(whole, whole),
        scratch_shapes=[small] * 2 + [
            vmem((chunks, size_x, size_y, LANES)),
            vmem((chunks, 3, size_x, seg) + tile),
            vmem((chunks, size_x) + tile),
            vmem((chunks, seg) + tile),
            vmem((chunks, seg) + tile),
            vmem((chunks, seg) + tile),
            vmem((seg,) + tile),
            vmem((chunks, 4, size_x, LANES)),
            vmem((chunks, 4, half, LANES)),
        ] + [pltpu.SemaphoreType.DMA((2,))] + [dma] * 7,
        compiler_params=pltpu.CompilerParams(collective_id=0, has_side_effects=True, vmem_limit_bytes=48 * 2**20),
    )(*[pltpu.with_memory_space_constraint(a, pltpu.HBM) for a in (density, extinction, sun_colour)])
    trans = jnp.exp(extinction[:, None, None] * column)
    return image + sky_colour[:, None, None] * trans, trans


def solution(mesh):
    return jax.shard_map(
        functools.partial(per_device, dict(mesh.shape)),
        mesh=mesh,
        in_specs=(P("light", "depth", "tile"), P(), P(), P()),
        out_specs=(P(None, ("light", "depth"), "tile"), P(None, ("light", "depth"), "tile")),
        check_vma=False,
    )
```

```python
import functools
import math

import jax
import jax.numpy as jnp
from jax import lax
from jax.experimental import pallas as pl
from jax.experimental.pallas import tpu as pltpu
from jax.sharding import PartitionSpec as P

LANES = 128
PARTS = 4
ROWS = 8
LOG2E = math.log2(math.e)
MESH = pl.DeviceIdType.MESH


def kernel(light_count, full_x, full_y, density, extinction_in, sun_in, image, column,
           extinction, sun_colour, dens, weight, front, own, chain_in, side_in, before, share, share_in,
           small_sem, load_sem, chain_send, chain_recv, side_send, side_recv, share_send, share_recv):
    chunks, size_x, size_y, _ = dens.shape
    seg = size_y // ROWS
    half = size_x // 2
    pair = 2 if light_count % 2 == 0 else 1
    length = light_count // pair
    light = lax.axis_index("light")
    depth = lax.axis_index("depth")
    level, side = light // pair, light % pair
    last = level == length - 1
    partner = light + 1 - 2 * side
    other = 1 - depth

    sends_chain = level < length - 1
    gets_chain = level > 0
    if pair == 2:
        sends_side = jnp.logical_or(side == 0, level > 0)
        gets_side = jnp.logical_or(side == 1, level > 0)

    def load(j):
        return pltpu.make_async_copy(density.at[:, :, pl.ds(j * LANES, LANES)], dens.at[j], load_sem.at[j])

    part = seg // PARTS
    messages = [(j, p) for j in range(chunks) for p in range(PARTS)]

    def steps(m):
        return m[0], pl.ds(m[1] * part, part)

    def chain(m):
        n = m[0] * PARTS + m[1]
        return pltpu.make_async_remote_copy(
            own.at[steps(m)], chain_in.at[steps(m)], chain_send.at[n], chain_recv.at[n],
            device_id={"light": light + pair}, device_id_type=MESH)

    def side_copy(m, source):
        n = m[0] * PARTS + m[1]
        return pltpu.make_async_remote_copy(
            source.at[steps(m)], side_in.at[steps(m)], side_send.at[n], side_recv.at[n],
            device_id={"light": partner}, device_id_type=MESH)

    def share_copy(j):
        return pltpu.make_async_remote_copy(
            share.at[j, :, pl.ds(pl.multiple_of(other * half, half), half)], share_in.at[j],
            share_send.at[j], share_recv.at[j],
            device_id={"depth": other}, device_id_type=MESH)

    for j in range(chunks):
        load(j).start()
    colours = [pltpu.make_async_copy(a, b, small_sem.at[i]) for i, (a, b) in enumerate(
        ((extinction_in, extinction), (sun_in, sun_colour)))]
    for copy in colours:
        copy.start()

    barrier = pltpu.get_barrier_semaphore()
    pl.semaphore_signal(barrier, inc=1, device_id={"depth": other}, device_id_type=MESH)
    if pair == 2:
        pl.semaphore_signal(barrier, inc=1, device_id={"light": partner}, device_id_type=MESH)

    @pl.when(sends_chain)
    def _():
        pl.semaphore_signal(barrier, inc=1, device_id={"light": light + pair}, device_id_type=MESH)

    @pl.when(gets_chain)
    def _():
        pl.semaphore_signal(barrier, inc=1, device_id={"light": light - pair}, device_id_type=MESH)

    pl.semaphore_wait(barrier, pair + jnp.minimum(level, 1) + jnp.minimum(length - 1 - level, 1))

    def cells(j, x):
        return [dens[j, x, pl.ds(s, ROWS, stride=seg), :] for s in range(seg)]

    def send_sums(m):
        @pl.when(sends_chain)
        def _():
            chain(m).start()

        if pair == 2:
            @pl.when(side == 0)
            def _():
                side_copy(m, own).start()

    for j in range(chunks):
        load(j).wait()

        def sums(x, total):
            d = cells(j, x)
            front[j, x] = functools.reduce(jnp.add, d)
            return tuple(t + v for t, v in zip(total, d))

        zero = jnp.zeros((ROWS, LANES), jnp.float32)
        total = lax.fori_loop(0, size_x, sums, (zero,) * seg, unroll=4)
        for s in range(seg):
            own[j, s] = total[s]

        @pl.when(level == 0)
        def _():
            for p in range(PARTS):
                send_sums((j, p))

    row = lax.broadcasted_iota(jnp.int32, (ROWS, LANES), 0)

    def shifted(v, n):
        return jnp.where(row >= n, pltpu.roll(v, n, 0), 0.0)

    def scan_group(g, carry):
        j, b = g // (size_x // ROWS), g % (size_x // ROWS)
        x0 = pl.multiple_of(b * ROWS, ROWS)
        group = front[j, pl.ds(x0, ROWS)]
        share[j, 3, pl.ds(x0, ROWS)] = jnp.sum(group, axis=1)
        for i in range(ROWS):
            v = shifted(group[i], 1)
            n = 1
            while n < ROWS:
                v = v + shifted(v, n)
                n *= 2
            front[j, x0 + i] = v
        return carry

    lax.fori_loop(0, chunks * (size_x // ROWS), scan_group, 0)

    for copy in colours:
        copy.wait()
    half_step = [extinction[c] * (-LOG2E / (2 * full_x)) for c in range(3)]
    view_step = [extinction[c] * (-LOG2E / full_y) for c in range(3)]
    sun_step = [extinction[c] * (-LOG2E / full_x) for c in range(3)]
    ratio = 2 * full_x // full_y
    squares = ratio.bit_length() - 1
    by_squares = ratio * full_y == 2 * full_x and ratio == 1 << squares and squares <= 3

    def weigh(j, carry):
        def step(x, lit):
            d = cells(j, x)
            e = front[j, x]
            after = []
            for c in range(3):
                seen = jnp.exp2(view_step[c] * e)
                for s in range(seg):
                    q = jnp.exp2(half_step[c] * d[s])
                    if by_squares:
                        a = q
                        for _ in range(squares):
                            a = a * a
                    else:
                        a = jnp.exp2(view_step[c] * d[s])
                    r = lit[c * seg + s] * q
                    after.append(r * q)
                    behind = seen * a
                    weight[j, c, x, s] = (seen - behind) * r
                    seen = behind
            return tuple(after)

        one = jnp.ones((ROWS, LANES), jnp.float32)
        lax.fori_loop(0, size_x, step, (one,) * (3 * seg), unroll=2)
        return carry

    early = jnp.minimum(level * chunks // max(length - 1, 1), chunks)
    lax.fori_loop(0, early, weigh, 0)

    @pl.when(gets_chain)
    def _():
        for m in messages:
            chain(m).wait_recv()
            if pair == 2:
                @pl.when(side == 1)
                def _():
                    side_copy(m, chain_in).start()
            own[steps(m)] = own[steps(m)] + chain_in[steps(m)]
            send_sums(m)

    lax.fori_loop(early, chunks, weigh, 0)

    def finish_rows(j, block):
        for c in range(3):
            g = [sun_colour[c] * jnp.exp2(sun_step[c] * before[s]) for s in range(seg)]
            for b in range(half // ROWS):
                x0 = block * half + b * ROWS
                parts = []
                for i in range(ROWS):
                    acc = weight[j, c, x0 + i, 0] * g[0]
                    for s in range(1, seg):
                        acc = acc + weight[j, c, x0 + i, s] * g[s]
                    parts.append(acc)
                share[j, c, pl.ds(pl.multiple_of(x0, ROWS), ROWS)] = jnp.sum(jnp.stack(parts), axis=1)

    def prepare(j):
        before[...] = jnp.zeros_like(before)

        @pl.when(gets_chain)
        def _():
            before[...] = chain_in[j]

        if pair == 2:
            @pl.when(gets_side)
            def _():
                for p in range(PARTS):
                    side_copy((j, p), own).wait_recv()
                before[...] = before[...] + side_in[j]

    def combine(j):
        share_copy(j).wait_recv()
        mine = pl.ds(pl.multiple_of(depth * half, half), half)
        lanes = pl.ds(j * LANES, LANES)
        near = depth == 0
        view, view_in = share[j, 3, mine], share_in[j, 3]
        view_front = jnp.where(near, view, view_in)
        for c in range(3):
            here, there = share[j, c, mine], share_in[j, c]
            first, second = jnp.where(near, here, there), jnp.where(near, there, here)
            image[c, :, lanes] = first + jnp.exp2(view_step[c] * view_front) * second
        column[:, lanes] = (view + view_in) * (-1.0 / full_y)

    for j in range(chunks):
        prepare(j)
        finish_rows(j, other)
        share_copy(j).start()
        finish_rows(j, depth)
    for j in range(chunks):
        combine(j)

    for j in range(chunks):
        share_copy(j).wait_send()

    @pl.when(sends_chain)
    def _():
        for m in messages:
            chain(m).wait_send()

    if pair == 2:
        @pl.when(sends_side)
        def _():
            for m in messages:
                side_copy(m, own).wait_send()


def per_device(mesh_shape, density, extinction, sun_colour, sky_colour):
    light_count, depth_count = mesh_shape["light"], mesh_shape["depth"]
    size_x, size_y, size_z = density.shape
    assert depth_count == 2
    chunks, seg, half = size_z // LANES, size_y // ROWS, size_x // 2
    out = jax.ShapeDtypeStruct((3, half, size_z), jnp.float32)
    vmem = functools.partial(pltpu.VMEM, dtype=jnp.float32)
    tile = (ROWS, LANES)
    dma = pltpu.SemaphoreType.DMA((chunks,))
    message = pltpu.SemaphoreType.DMA((chunks * PARTS,))
    hbm = pl.BlockSpec(memory_space=pltpu.HBM)
    small = pltpu.SMEM((3,), jnp.float32)
    whole = pl.BlockSpec(memory_space=pltpu.VMEM)
    image, column = pl.pallas_call(
        functools.partial(kernel, light_count, size_x * light_count, size_y * depth_count),
        out_shape=(out, jax.ShapeDtypeStruct((half, size_z), jnp.float32)),
        in_specs=[hbm] * 3,
        out_specs=(whole, whole),
        scratch_shapes=[small] * 2 + [
            vmem((chunks, size_x, size_y, LANES)),
            vmem((chunks, 3, size_x, seg) + tile),
            vmem((chunks, size_x) + tile),
            vmem((chunks, seg) + tile),
            vmem((chunks, seg) + tile),
            vmem((chunks, seg) + tile),
            vmem((seg,) + tile),
            vmem((chunks, 4, size_x, LANES)),
            vmem((chunks, 4, half, LANES)),
        ] + [pltpu.SemaphoreType.DMA((2,))] + [dma] + [message] * 4 + [dma] * 2,
        compiler_params=pltpu.CompilerParams(collective_id=0, has_side_effects=True, vmem_limit_bytes=48 * 2**20),
    )(*[pltpu.with_memory_space_constraint(a, pltpu.HBM) for a in (density, extinction, sun_colour)])
    trans = jnp.exp(extinction[:, None, None] * column)
    return image + sky_colour[:, None, None] * trans, trans


def solution(mesh):
    return jax.shard_map(
        functools.partial(per_device, dict(mesh.shape)),
        mesh=mesh,
        in_specs=(P("light", "depth", "tile"), P(), P(), P()),
        out_specs=(P(None, ("light", "depth"), "tile"), P(None, ("light", "depth"), "tile")),
        check_vma=False,
    )
```

```python
import functools
import math

import jax
import jax.numpy as jnp
from jax import lax
from jax.experimental import pallas as pl
from jax.experimental.pallas import tpu as pltpu
from jax.sharding import PartitionSpec as P

LANES = 128
PARTS = 2
ROWS = 8
LOG2E = math.log2(math.e)
MESH = pl.DeviceIdType.MESH


def kernel(light_count, full_x, full_y, density, extinction_in, sun_in, image, column,
           extinction, sun_colour, dens, weight, front, own, chain_in, side_in, before, share, share_in,
           small_sem, load_sem, chain_send, chain_recv, side_send, side_recv, share_send, share_recv):
    chunks, size_x, size_y, _ = dens.shape
    seg = size_y // ROWS
    half = size_x // 2
    pair = 2 if light_count % 2 == 0 else 1
    length = light_count // pair
    light = lax.axis_index("light")
    depth = lax.axis_index("depth")
    level, side = light // pair, light % pair
    last = level == length - 1
    partner = light + 1 - 2 * side
    other = 1 - depth

    sends_chain = level < length - 1
    gets_chain = level > 0
    if pair == 2:
        sends_side = jnp.logical_or(side == 0, level > 0)
        gets_side = jnp.logical_or(side == 1, level > 0)

    def load(j):
        return pltpu.make_async_copy(density.at[:, :, pl.ds(j * LANES, LANES)], dens.at[j], load_sem.at[j])

    part = seg // PARTS
    messages = [(j, p) for j in range(chunks) for p in range(PARTS)]

    def steps(m):
        return m[0], pl.ds(m[1] * part, part)

    def chain(m):
        n = m[0] * PARTS + m[1]
        return pltpu.make_async_remote_copy(
            own.at[steps(m)], chain_in.at[steps(m)], chain_send.at[n], chain_recv.at[n],
            device_id={"light": light + pair}, device_id_type=MESH)

    def side_copy(m, source):
        n = m[0] * PARTS + m[1]
        return pltpu.make_async_remote_copy(
            source.at[steps(m)], side_in.at[steps(m)], side_send.at[n], side_recv.at[n],
            device_id={"light": partner}, device_id_type=MESH)

    def share_copy(j):
        return pltpu.make_async_remote_copy(
            share.at[j, :, pl.ds(pl.multiple_of(other * half, half), half)], share_in.at[j],
            share_send.at[j], share_recv.at[j],
            device_id={"depth": other}, device_id_type=MESH)

    for j in range(chunks):
        load(j).start()
    colours = [pltpu.make_async_copy(a, b, small_sem.at[i]) for i, (a, b) in enumerate(
        ((extinction_in, extinction), (sun_in, sun_colour)))]
    for copy in colours:
        copy.start()

    barrier = pltpu.get_barrier_semaphore()
    pl.semaphore_signal(barrier, inc=1, device_id={"depth": other}, device_id_type=MESH)
    if pair == 2:
        pl.semaphore_signal(barrier, inc=1, device_id={"light": partner}, device_id_type=MESH)

    @pl.when(sends_chain)
    def _():
        pl.semaphore_signal(barrier, inc=1, device_id={"light": light + pair}, device_id_type=MESH)

    @pl.when(gets_chain)
    def _():
        pl.semaphore_signal(barrier, inc=1, device_id={"light": light - pair}, device_id_type=MESH)

    pl.semaphore_wait(barrier, pair + jnp.minimum(level, 1) + jnp.minimum(length - 1 - level, 1))

    def cells(j, x):
        return [dens[j, x, pl.ds(s, ROWS, stride=seg), :] for s in range(seg)]

    def send_sums(m):
        @pl.when(sends_chain)
        def _():
            chain(m).start()

        if pair == 2:
            @pl.when(side == 0)
            def _():
                side_copy(m, own).start()

    for j in range(chunks):
        load(j).wait()

        def sums(x, total):
            d = cells(j, x)
            front[j, x] = functools.reduce(jnp.add, d)
            return tuple(t + v for t, v in zip(total, d))

        zero = jnp.zeros((ROWS, LANES), jnp.float32)
        total = lax.fori_loop(0, size_x, sums, (zero,) * seg, unroll=4)
        for s in range(seg):
            own[j, s] = total[s]

        @pl.when(level == 0)
        def _():
            for p in range(PARTS):
                send_sums((j, p))

    row = lax.broadcasted_iota(jnp.int32, (ROWS, LANES), 0)

    def shifted(v, n):
        return jnp.where(row >= n, pltpu.roll(v, n, 0), 0.0)

    def scan_group(g, carry):
        j, b = g // (size_x // ROWS), g % (size_x // ROWS)
        x0 = pl.multiple_of(b * ROWS, ROWS)
        group = front[j, pl.ds(x0, ROWS)]
        share[j, 3, pl.ds(x0, ROWS)] = jnp.sum(group, axis=1)
        for i in range(ROWS):
            v = shifted(group[i], 1)
            n = 1
            while n < ROWS:
                v = v + shifted(v, n)
                n *= 2
            front[j, x0 + i] = v
        return carry

    lax.fori_loop(0, chunks * (size_x // ROWS), scan_group, 0, unroll=4)

    for copy in colours:
        copy.wait()
    half_step = [extinction[c] * (-LOG2E / (2 * full_x)) for c in range(3)]
    view_step = [extinction[c] * (-LOG2E / full_y) for c in range(3)]
    sun_step = [extinction[c] * (-LOG2E / full_x) for c in range(3)]
    ratio = 2 * full_x // full_y
    squares = ratio.bit_length() - 1
    by_squares = ratio * full_y == 2 * full_x and ratio == 1 << squares and squares <= 3

    def weigh(j, carry):
        one = jnp.ones((ROWS, LANES), jnp.float32)
        for c in range(3):
            def step(x, lit):
                d = cells(j, x)
                seen = jnp.exp2(view_step[c] * front[j, x])
                after = []
                for s in range(seg):
                    q = jnp.exp2(half_step[c] * d[s])
                    if by_squares:
                        a = q
                        for _ in range(squares):
                            a = a * a
                    else:
                        a = jnp.exp2(view_step[c] * d[s])
                    r = lit[s] * q
                    after.append(r * q)
                    behind = seen * a
                    weight[j, c, x, s] = (seen - behind) * r
                    seen = behind
                return tuple(after)

            lax.fori_loop(0, size_x, step, (one,) * seg, unroll=4)
        return carry

    early = jnp.minimum(level * chunks // max(length - 1, 1), chunks)
    lax.fori_loop(0, early, weigh, 0)

    @pl.when(gets_chain)
    def _():
        for m in messages:
            chain(m).wait_recv()
            if pair == 2:
                @pl.when(side == 1)
                def _():
                    side_copy(m, chain_in).start()
            own[steps(m)] = own[steps(m)] + chain_in[steps(m)]
            send_sums(m)

    lax.fori_loop(early, chunks, weigh, 0)

    def finish_rows(j, block):
        for c in range(3):
            g = [sun_colour[c] * jnp.exp2(sun_step[c] * before[s]) for s in range(seg)]
            for b in range(half // ROWS):
                x0 = block * half + b * ROWS
                parts = []
                for i in range(ROWS):
                    acc = weight[j, c, x0 + i, 0] * g[0]
                    for s in range(1, seg):
                        acc = acc + weight[j, c, x0 + i, s] * g[s]
                    parts.append(acc)
                share[j, c, pl.ds(pl.multiple_of(x0, ROWS), ROWS)] = jnp.sum(jnp.stack(parts), axis=1)

    def prepare(j):
        before[...] = jnp.zeros_like(before)

        @pl.when(gets_chain)
        def _():
            before[...] = chain_in[j]

        if pair == 2:
            @pl.when(gets_side)
            def _():
                for p in range(PARTS):
                    side_copy((j, p), own).wait_recv()
                before[...] = before[...] + side_in[j]

    def combine(j):
        share_copy(j).wait_recv()
        mine = pl.ds(pl.multiple_of(depth * half, half), half)
        lanes = pl.ds(j * LANES, LANES)
        near = depth == 0
        view, view_in = share[j, 3, mine], share_in[j, 3]
        view_front = jnp.where(near, view, view_in)
        for c in range(3):
            here, there = share[j, c, mine], share_in[j, c]
            first, second = jnp.where(near, here, there), jnp.where(near, there, here)
            image[c, :, lanes] = first + jnp.exp2(view_step[c] * view_front) * second
        column[:, lanes] = (view + view_in) * (-1.0 / full_y)

    for j in range(chunks):
        prepare(j)
        finish_rows(j, other)
        share_copy(j).start()
        finish_rows(j, depth)
    for j in range(chunks):
        combine(j)

    for j in range(chunks):
        share_copy(j).wait_send()

    @pl.when(sends_chain)
    def _():
        for m in messages:
            chain(m).wait_send()

    if pair == 2:
        @pl.when(sends_side)
        def _():
            for m in messages:
                side_copy(m, own).wait_send()


def per_device(mesh_shape, density, extinction, sun_colour, sky_colour):
    light_count, depth_count = mesh_shape["light"], mesh_shape["depth"]
    size_x, size_y, size_z = density.shape
    assert depth_count == 2
    chunks, seg, half = size_z // LANES, size_y // ROWS, size_x // 2
    out = jax.ShapeDtypeStruct((3, half, size_z), jnp.float32)
    vmem = functools.partial(pltpu.VMEM, dtype=jnp.float32)
    tile = (ROWS, LANES)
    dma = pltpu.SemaphoreType.DMA((chunks,))
    message = pltpu.SemaphoreType.DMA((chunks * PARTS,))
    hbm = pl.BlockSpec(memory_space=pltpu.HBM)
    small = pltpu.SMEM((3,), jnp.float32)
    whole = pl.BlockSpec(memory_space=pltpu.VMEM)
    image, column = pl.pallas_call(
        functools.partial(kernel, light_count, size_x * light_count, size_y * depth_count),
        out_shape=(out, jax.ShapeDtypeStruct((half, size_z), jnp.float32)),
        in_specs=[hbm] * 3,
        out_specs=(whole, whole),
        scratch_shapes=[small] * 2 + [
            vmem((chunks, size_x, size_y, LANES)),
            vmem((chunks, 3, size_x, seg) + tile),
            vmem((chunks, size_x) + tile),
            vmem((chunks, seg) + tile),
            vmem((chunks, seg) + tile),
            vmem((chunks, seg) + tile),
            vmem((seg,) + tile),
            vmem((chunks, 4, size_x, LANES)),
            vmem((chunks, 4, half, LANES)),
        ] + [pltpu.SemaphoreType.DMA((2,))] + [dma] + [message] * 4 + [dma] * 2,
        compiler_params=pltpu.CompilerParams(collective_id=0, has_side_effects=True, vmem_limit_bytes=48 * 2**20),
    )(*[pltpu.with_memory_space_constraint(a, pltpu.HBM) for a in (density, extinction, sun_colour)])
    trans = jnp.exp(extinction[:, None, None] * column)
    return image + sky_colour[:, None, None] * trans, trans


def solution(mesh):
    return jax.shard_map(
        functools.partial(per_device, dict(mesh.shape)),
        mesh=mesh,
        in_specs=(P("light", "depth", "tile"), P(), P(), P()),
        out_specs=(P(None, ("light", "depth"), "tile"), P(None, ("light", "depth"), "tile")),
        check_vma=False,
    )
```
